32 devices in a mesh: sub: 8 (over z, x), grp: 4 (over y, core).
Axes of the slice: x: 2, y: 2, z: 4, core: 2. Of those that a mesh axis runs over, the one named last changes fastest.
Arguments:
- rhs_field: bfloat16 [8, 4, 1024, 256], P('sub', 'grp'), may hold values from -6 to 6
- local_inverse: bfloat16 [8, 4, 1024, 1024], P('sub', 'grp'), may hold values from -0.03125 to 0.03125
- stiff_diag: float32 [8, 4, 1024], P('sub', 'grp'), may hold values from 1 to 3
- bonds: float32 [8, 4, 1024], P('sub', 'grp'), may hold values from 0.1 to 0.4
- deflation: bfloat16 [8, 4, 1024, 64], P('sub', 'grp'), as said below
- margin_rows: int32 [8, 4, 4, 128], P('sub', 'grp'), may hold values from 0 to 1023, as said below
- margin_count: int32 [8, 4, 4], P('sub', 'grp'), may hold values from 64 to 128, as said below
Outputs:
- solution: float32 [8, 4, 1024, 256], P('sub', 'grp')
- residual: bfloat16 [8, 4, 1024, 256], P('sub', 'grp')
The draws below stay inside these ranges and needn't reach their ends.
Inputs may be any that keep to these rules, and one draw needn't show every extreme that they name: `margin_rows`: within one subdomain and direction the 128 row numbers are distinct. `margin_count`: A subdomain's count toward a neighbour equals that neighbour's count toward it in the opposite direction. `deflation`: entries have magnitude at most 6 / sqrt(1024).
All inputs are finite; a program needn't handle non-finite values.
Results may differ from the reference program's by a relative error of at most 0.0026.
Values sent between devices are 32-bit elements; how exact they have to be, the bound alone decides.
A program may use at most 64 MiB of HBM per device.

```python
import math
import jax
import jax.numpy as jnp
from jax import lax

NODES = 1024
DEFL = 64
MARGIN = 128
RHS = 256
ITERS = 2
SUBS = 8
GROUPS = 4


def margin_layout(key):
    base_key = jax.random.fold_in(key, 7)
    keyring = jax.random.split(base_key, SUBS * GROUPS * 4)

    def one_list(single):
        return jax.random.permutation(single, NODES)[:MARGIN]
    row_lists = jax.vmap(one_list)(keyring)
    return row_lists.reshape(SUBS, GROUPS, 4, MARGIN).astype(jnp.int32)


def draw_margin_rows(key, part):
    return margin_layout(key)


def draw_margin_count(key, part):
    base_key = jax.random.fold_in(key, 13)
    edge_sub = jax.random.randint(jax.random.fold_in(base_key, 1), (SUBS + 1, GROUPS), MARGIN // 2, MARGIN + 1)
    edge_sub = edge_sub.at[1, 0].set(MARGIN)
    edge_grp = jax.random.randint(jax.random.fold_in(base_key, 2), (SUBS, GROUPS + 1), MARGIN // 2, MARGIN + 1)
    edge_grp = edge_grp.at[0, 1].set(MARGIN // 2)
    stacked = jnp.stack([edge_sub[:-1], edge_sub[1:], edge_grp[:, :-1], edge_grp[:, 1:]], axis=-1)
    return stacked.astype(jnp.int32)


def base_values(key, shape):
    values = jnp.clip(jax.random.normal(key, shape, jnp.float32), -6.0, 6.0)
    return values / jnp.sqrt(jnp.float32(NODES))


def set_one(target, places, amount):
    return target.at[places].set(amount)


def draw_deflation(key, part):
    row_sets = margin_layout(key)
    base_key = jax.random.fold_in(key, 29)
    field = base_values(jax.random.fold_in(base_key, 1), (SUBS, GROUPS, NODES, DEFL))
    edge_sub = base_values(jax.random.fold_in(base_key, 2), (SUBS + 1, GROUPS, MARGIN, DEFL))
    edge_grp = base_values(jax.random.fold_in(base_key, 3), (SUBS, GROUPS + 1, MARGIN, DEFL))
    shared = [edge_sub[:-1], edge_sub[1:], edge_grp[:, :-1], edge_grp[:, 1:]]
    setter = jax.vmap(jax.vmap(set_one))
    for direction in range(4):
        field = setter(field, row_sets[:, :, direction], shared[direction])
    return field.astype(jnp.bfloat16)


def block_scale(own_key, dims, cuts, smallest, largest):
    gain = 1.0
    for position, blocks in cuts:
        steps = jax.random.uniform(jax.random.fold_in(jax.random.fold_in(own_key, 6), position), (blocks,), jnp.float32, smallest / len(cuts), largest / len(cuts))
        gain = gain * jnp.repeat(jnp.exp(steps), dims[position] // blocks).reshape((-1,) + (1,) * (len(dims) - 1 - position))
    return gain


def bell_draw(rng, extent, width, bound, pieces=(), kind=jnp.bfloat16):
    result = width * jax.random.normal(rng, extent, jnp.float32)
    if pieces:
        result = result * block_scale(rng, extent, pieces, -0.22, 0.18)
    return jnp.clip(result, -bound, bound).astype(kind)


def setup_inputs(seed: int = 0) -> dict:
    streams_of = jax.random.split(jax.random.key(seed), 8)
    rhs_field = bell_draw(streams_of[0], (SUBS, GROUPS, NODES, RHS), 1.0, 6.0, ((0, 8), (1, 4)))
    local_inverse = bell_draw(streams_of[1], (SUBS, GROUPS, NODES, NODES), (40 * NODES) ** -0.5, 0.03125, ((0, 8), (1, 4)))
    stiff_diag = jnp.clip(jnp.exp(math.log(3.0) - 1.0986123 * jax.random.uniform(streams_of[2], (SUBS, GROUPS, NODES), jnp.float32) ** block_scale(streams_of[2], (SUBS, GROUPS, NODES), ((0, 8), (1, 4)), -0.2, 0.2)), 1.0, 3.0)
    bonds = jnp.clip(0.1 + 0.3 * jax.random.uniform(streams_of[3], (SUBS, GROUPS, NODES), jnp.float32) ** block_scale(streams_of[3], (SUBS, GROUPS, NODES), ((0, 8), (1, 4)), -0.2, 0.2), 0.1, 0.4)
    deflation = draw_deflation(jax.random.fold_in(streams_of[7], 71), 0)
    margin_rows = draw_margin_rows(jax.random.fold_in(streams_of[7], 71), 0)
    margin_count = draw_margin_count(jax.random.fold_in(streams_of[7], 71), 0)
    return {"rhs_field": rhs_field, "local_inverse": local_inverse, "stiff_diag": stiff_diag, "bonds": bonds, "deflation": deflation, "margin_rows": margin_rows, "margin_count": margin_count}


CHEB_FIRST = 0.4
CHEB_SECOND = 0.3
COUPLE_WEIGHT = 0.5


def from_neighbours(payloads):
    zero_sub = jnp.zeros_like(payloads[0][:1])
    zero_grp = jnp.zeros_like(payloads[0][:, :1])
    arrived = [jnp.concatenate([zero_sub, payloads[1][:-1]], 0),
               jnp.concatenate([payloads[0][1:], zero_sub], 0),
               jnp.concatenate([zero_grp, payloads[3][:, :-1]], 1),
               jnp.concatenate([payloads[2][:, 1:], zero_grp], 1)]
    return arrived


def scatter_one(target, places, amount):
    return target.at[places].add(amount)


def margin_sum(field, margin_rows, margin_count):
    payloads = [jnp.take_along_axis(field, margin_rows[:, :, direction, :, None], axis=2) for direction in range(4)]
    arrived = from_neighbours(payloads)
    live = jnp.arange(margin_rows.shape[3])
    scatter_all = jax.vmap(jax.vmap(scatter_one))
    total = jnp.zeros_like(field)
    for direction in range(4):
        masked = (live[None, None, :] < margin_count[:, :, direction, None]).astype(jnp.float32)[..., None]
        total = scatter_all(total, margin_rows[:, :, direction], arrived[direction] * masked)
    return total


def local_op(field, stiff_diag, bonds):
    diag_col = stiff_diag[..., None]
    bond_col = bonds[..., None]
    zero_row = jnp.zeros_like(field[:, :, :1])
    shifted_down = jnp.concatenate([zero_row, field[:, :, :-1]], 2)
    weighted = bond_col * field
    upper_part = jnp.concatenate([weighted[:, :, 1:], zero_row], 2)
    return diag_col * field - bond_col * shifted_down - upper_part


def apply_global(field, stiff_diag, bonds, margin_rows, margin_count):
    return local_op(field, stiff_diag, bonds) - COUPLE_WEIGHT * margin_sum(field, margin_rows, margin_count)


def per_device_dot(pair):
    return jnp.dot(pair[0], pair[1], preferred_element_type=jnp.float32)


def per_device_tdot(pair):
    return jnp.dot(pair[0].T, pair[1], preferred_element_type=jnp.float32)


def reference(rhs_field, local_inverse, stiff_diag, bonds, deflation, margin_rows, margin_count):
    subs, groups, nodes, columns = rhs_field.shape
    defl = deflation.shape[3]
    flat_inverse = local_inverse.reshape(subs * groups, nodes, nodes)
    flat_basis = deflation.reshape(subs * groups, nodes, defl)
    basis_wide = deflation.astype(jnp.float32)
    hp = lax.Precision.HIGHEST
    solution = jnp.zeros(rhs_field.shape, jnp.float32)
    residual = rhs_field.astype(jnp.float32)
    for sweep in range(ITERS):
        half = residual.astype(jnp.bfloat16)
        flat_half = half.reshape(subs * groups, nodes, columns)
        coarse = lax.map(per_device_tdot, (flat_basis, flat_half)).reshape(subs, groups, defl, columns)
        first = CHEB_FIRST * coarse
        lifted = jnp.einsum("sgnm,sgmr->sgnr", basis_wide, first, precision=hp)
        pushed = apply_global(lifted, stiff_diag, bonds, margin_rows, margin_count)
        applied = jnp.einsum("sgnm,sgnr->sgmr", basis_wide, pushed, precision=hp)
        second = first + CHEB_SECOND * (coarse - applied)
        dense = lax.map(per_device_dot, (flat_inverse, flat_half)).reshape(subs, groups, nodes, columns)
        correction = residual / stiff_diag[..., None] + dense + jnp.einsum("sgnm,sgmr->sgnr", basis_wide, second, precision=hp)
        summed = correction + margin_sum(correction, margin_rows, margin_count)
        solution = solution + summed
        residual = residual - apply_global(summed, stiff_diag, bonds, margin_rows, margin_count)
    return solution, residual.astype(jnp.bfloat16)
```

```python
import functools

import jax
import jax.numpy as jnp
from jax import lax
from jax.experimental import pallas as pl
from jax.experimental.pallas import tpu as pltpu
from jax.sharding import PartitionSpec as P

ITERS = 2
CHUNKS = 2

CHEB_FIRST = 0.4
CHEB_SECOND = 0.3
COUPLE_WEIGHT = 0.5

MESH = pl.DeviceIdType.MESH
F32 = jnp.float32
BF16 = jnp.bfloat16
NT = (((1,), (1,)), ((), ()))
SUB, GRP, ALL = (0, 1), (2, 3), (0, 1, 2, 3)


def dot(a, b):
    return jnp.dot(a, b, preferred_element_type=F32)


def dot_nt(a, b):
    return lax.dot_general(a, b, NT, preferred_element_type=F32)


def pair(x):
    high = x.astype(BF16)
    low = (x - high.astype(F32)).astype(BF16)
    return jnp.concatenate([high, low], axis=1)


def fold(x):
    width = x.shape[1] // 2
    return x[:, :width] + x[:, width:]


def one_hot(hit):
    return jnp.where(hit, 1.0, 0.0).astype(BF16)


def upright(row):
    size = row.shape[1]
    return jnp.broadcast_to(row, (size, size)).T


def kernel(
    subs, groups,
    rhs_hbm, inverse_hbm, diag_row, bond_row, basis_t, rows, count,
    sol_out, res_out,
    rhs, inverse, basis, gather, scatter, cross, edge_basis, edge_cols, tiles, own_tile,
    diag, inv_diag, bond_low, bond_high,
    resid, corr, total, own_part, pulled, second, came,
    edge_out, edge_in, coarse_out, coarse_in, margin_out, margin_in,
    rhs_sem, load_sem, edge_send, edge_recv, send_sem, recv_sem,
):
    nodes, columns = rhs.shape
    defl = basis_t.shape[0]
    margin = rows.shape[1]
    width = columns // CHUNKS
    side = 2 * margin
    s, g = lax.axis_index("sub"), lax.axis_index("grp")
    has = [s > 0, s < subs - 1, g > 0, g < groups - 1]
    near = [(s - 1, g), (s + 1, g), (s, g - 1), (s, g + 1)]

    rhs_load = pltpu.make_async_copy(rhs_hbm, rhs, rhs_sem)
    rhs_load.start()

    barrier = pltpu.get_barrier_semaphore()
    for d in range(4):
        @pl.when(has[d])
        def _(d=d):
            pl.semaphore_signal(barrier, inc=1, device_id=near[d], device_id_type=MESH)

    def edge_copy(d):
        return pltpu.make_async_remote_copy(
            src_ref=edge_out.at[d], dst_ref=edge_in.at[d ^ 1],
            send_sem=edge_send.at[d], recv_sem=edge_recv.at[d ^ 1],
            device_id=near[d], device_id_type=MESH)

    def coarse_copy(t, h, d):
        return pltpu.make_async_remote_copy(
            src_ref=coarse_out.at[t, h], dst_ref=coarse_in.at[t, h, d ^ 1],
            send_sem=send_sem.at[t, h, 2, d], recv_sem=recv_sem.at[t, h, 2, d ^ 1],
            device_id=near[d], device_id_type=MESH)

    def margin_copy(t, h, p, d):
        return pltpu.make_async_remote_copy(
            src_ref=margin_out.at[t, h, p, d], dst_ref=margin_in.at[t, h, p, d ^ 1],
            send_sem=send_sem.at[t, h, p, d], recv_sem=recv_sem.at[t, h, p, d ^ 1],
            device_id=near[d], device_id_type=MESH)

    def start(copy_to, dirs=ALL):
        for d in dirs:
            @pl.when(has[d])
            def _(d=d):
                copy_to(d).start()

    def arrive(copy_to, dirs=ALL):
        for d in dirs:
            @pl.when(has[d])
            def _(d=d):
                copy_to(d ^ 1).wait_recv()

    def sent(copy_to):
        for d in range(4):
            @pl.when(has[d])
            def _(d=d):
                copy_to(d).wait_send()

    def cols(h):
        return pl.ds(h * width, width)

    def block(k):
        return pl.ds(k * side, side)

    row_values = rows[...].astype(F32)
    lane = lax.broadcasted_iota(jnp.int32, (margin, margin), 1).astype(F32)
    tall = []
    for d in range(4):
        tall.append(upright(row_values[d:d + 1]))
        for j in range(nodes // margin):
            gather[pl.ds(d * margin, margin), pl.ds(j * margin, margin)] = one_hot(tall[d] == lane + float(j * margin))
    edges = dot_nt(basis_t[...], gather[...])
    for d in range(4):
        edge_out[d] = edges[:, d * margin:(d + 1) * margin]
    rhs_load.wait()
    load = pltpu.make_async_copy(inverse_hbm, inverse, load_sem)
    load.start()
    first = dot(basis_t[...], rhs[...])
    for h in range(CHUNKS):
        coarse_out[0, h] = first[:, h * width:(h + 1) * width]

    pl.semaphore_wait(barrier, sum(h.astype(jnp.int32) for h in has))
    start(edge_copy)
    for h in range(CHUNKS):
        start(functools.partial(coarse_copy, 0, h))

    for d in range(4):
        @pl.when(jnp.logical_not(has[d]))
        def _(d=d):
            edge_in[d] = jnp.zeros_like(edge_in[d])
            for t in range(ITERS):
                for h in range(CHUNKS):
                    coarse_in[t, h, d] = jnp.zeros_like(coarse_in[t, h, d])
                    for p in range(2):
                        margin_in[t, h, p, d] = jnp.zeros_like(margin_in[t, h, p, d])

    basis[...] = basis_t[...].astype(F32).T.astype(BF16)
    edge_basis[...] = dot(gather[...], basis[...]).astype(BF16)
    for j in range(nodes // margin):
        part = pl.ds(j * margin, margin)
        tall_diag = upright(diag_row[:, j * margin:(j + 1) * margin])
        diag[part, :] = tall_diag
        inv_diag[part, :] = 1.0 / tall_diag
        bond_low[part, :] = upright(bond_row[:, j * margin:(j + 1) * margin])
    node = lax.broadcasted_iota(jnp.int32, (nodes, margin), 0).astype(F32)
    bonds = bond_low[...]
    bond_high[...] = jnp.where(node == float(nodes - 1), 0.0, pltpu.roll(bonds, nodes - 1, 0))
    bond_low[...] = jnp.where(node == 0.0, 0.0, bonds)

    def local_op(x):
        lanes = x.shape[1]
        return (diag[:, :lanes] * x - bond_low[:, :lanes] * pltpu.roll(x, 1, 0)
                - bond_high[:, :lanes] * pltpu.roll(x, nodes - 1, 0))

    def correct(t, h):
        wide = resid[:, cols(h)]
        value = corr[:, cols(h)] + wide * inv_diag[...]
        corr[:, cols(h)] = value
        taken = fold(dot(gather[...], pair(value)))
        for d in range(4):
            margin_out[t, h, 0, d] = taken[d * margin:(d + 1) * margin]

    load.wait()
    corr[...] = dot(inverse[...], rhs[...])
    for h in range(CHUNKS):
        resid[:, cols(h)] = rhs[:, h * width:(h + 1) * width].astype(F32)
        correct(0, h)

    live = []
    spot = lax.broadcasted_iota(jnp.int32, (1, margin), 1)
    for d in range(4):
        live.append(spot < jnp.where(has[d], count[d], 0))
    for d in range(4):
        target = jnp.where(live[d], row_values[d:d + 1], -1.0)
        scatter[:, d * margin:(d + 1) * margin] = one_hot(node == target)
        for e in range(4):
            cross[pl.ds(e * margin, margin), pl.ds(d * margin, margin)] = one_hot(tall[e] == target)
        edge_cols[:, d * margin:(d + 1) * margin] = jnp.where(live[d], edge_out[d], 0.0).astype(BF16)

    def keep_stacked(ref, value):
        high = value.astype(BF16)
        ref[:defl] = high
        ref[defl:] = (value - high.astype(F32)).astype(BF16)

    def apply_stacked(ref, parts):
        both = dot(ref[...], parts)
        return fold(both[:defl]) + both[defl:, :width]

    pushed = pair(local_op(basis[...].astype(F32)))
    own = fold(dot(basis_t[...], pushed))
    eye = (lax.broadcasted_iota(jnp.int32, (defl, defl), 0)
           == lax.broadcasted_iota(jnp.int32, (defl, defl), 1)).astype(F32)
    keep_stacked(own_tile, (CHEB_FIRST + CHEB_SECOND) * eye - CHEB_FIRST * CHEB_SECOND * own)
    for h in range(CHUNKS):
        own_part[h] = apply_stacked(own_tile, pair(coarse_out[0, h]))

    arrive(edge_copy)
    scale = CHEB_FIRST * CHEB_SECOND * COUPLE_WEIGHT
    keep_stacked(tiles, jnp.concatenate([
        scale * dot_nt(edge_cols[:, d * margin:(d + 1) * margin], edge_in[d].astype(BF16)) for d in range(4)], axis=1))

    def send_margin(t, h):
        arrive(functools.partial(coarse_copy, t, h), GRP)
        arrive(functools.partial(coarse_copy, t, h), SUB)
        parts = pair(own_part[h] + apply_stacked(tiles, pair(coarse_in[t, h].reshape(4 * defl, width))))
        second[h] = parts
        for k, dirs in enumerate((SUB, GRP)):
            taken = fold(dot(edge_basis[block(k), :], parts))
            for d in dirs:
                margin_out[t, h, 0, d] = margin_out[t, h, 0, d] + taken[(d % 2) * margin:(d % 2 + 1) * margin]
            start(functools.partial(margin_copy, t, h, 0), dirs)

    def lift(h):
        corr[:, cols(h)] = corr[:, cols(h)] + fold(dot(basis[...], second[h]))

    def take(t, h, p, k):
        arrive(functools.partial(margin_copy, t, h, p), (SUB, GRP)[k])
        parts = pair(margin_in[t, h, p, 2 * k:2 * k + 2].reshape(side, width))
        came[h, block(k), :] = parts
        return parts

    def send_summed(t, h):
        taken = fold(dot(cross[:, side:], take(t, h, 0, 1)))
        for d in range(4):
            margin_out[t, h, 1, d] = margin_out[t, h, 0, d] + taken[d * margin:(d + 1) * margin]
        parts = take(t, h, 0, 0)
        for k, dirs in enumerate((SUB, GRP)):
            taken = fold(dot(cross[block(k), :side], parts))
            for d in dirs:
                margin_out[t, h, 1, d] = margin_out[t, h, 1, d] + taken[(d % 2) * margin:(d % 2 + 1) * margin]
            start(functools.partial(margin_copy, t, h, 1), dirs)

    def add_up(t, h):
        summed = corr[:, cols(h)] + fold(dot(scatter[...], came[h]))
        if t == 0:
            total[:, cols(h)] = summed
        else:
            total[:, cols(h)] = total[:, cols(h)] + summed
        if t == ITERS - 1:
            sol_out[:, cols(h)] = total[:, cols(h)]
        value = resid[:, cols(h)] - local_op(summed)
        resid[:, cols(h)] = value
        if t < ITERS - 1:
            pulled[h] = fold(dot(basis_t[...], pair(value)))

    def send_coarse(t, h):
        take(t, h, 1, 1)
        take(t, h, 1, 0)
        value = pulled[h] + COUPLE_WEIGHT * fold(dot(edge_cols[...], came[h]))
        coarse_out[t + 1, h] = value
        start(functools.partial(coarse_copy, t + 1, h))

    def renew(t, h):
        own_part[h] = apply_stacked(own_tile, pair(coarse_out[t, h]))
        value = resid[:, cols(h)] + COUPLE_WEIGHT * fold(dot(scatter[...], came[h]))
        resid[:, cols(h)] = value
        corr[:, cols(h)] = dot(inverse[...], value.astype(BF16))
        correct(t, h)

    for t in range(ITERS):
        for h in range(CHUNKS):
            send_margin(t, h)
            if t > 0 and h == 0:
                renew(t, CHUNKS - 1)
            lift(h)
        for h in range(CHUNKS):
            send_summed(t, h)
            add_up(t, h)
        for h in range(CHUNKS):
            if t < ITERS - 1:
                send_coarse(t, h)
                if h < CHUNKS - 1:
                    renew(t + 1, h)
            else:
                parts = take(t, h, 1, 1)
                resid[:, cols(h)] = resid[:, cols(h)] + COUPLE_WEIGHT * fold(dot(scatter[:, side:], parts))
                parts = take(t, h, 1, 0)
                res_out[:, cols(h)] = (
                    resid[:, cols(h)] + COUPLE_WEIGHT * fold(dot(scatter[:, :side], parts))).astype(BF16)

    sent(edge_copy)
    for t in range(ITERS):
        for h in range(CHUNKS):
            sent(functools.partial(coarse_copy, t, h))
            for p in range(2):
                sent(functools.partial(margin_copy, t, h, p))


def put_out(sol_in, res_in, sol_out, res_out, sem):
    copies = [pltpu.make_async_copy(sol_in, sol_out, sem.at[0]), pltpu.make_async_copy(res_in, res_out, sem.at[1])]
    for copy in copies:
        copy.start()
    for copy in copies:
        copy.wait()


def per_device(mesh, rhs_field, local_inverse, stiff_diag, bonds, deflation, margin_rows, margin_count):
    nodes, columns = rhs_field.shape[2:]
    defl = deflation.shape[3]
    margin = margin_rows.shape[3]
    width = columns // CHUNKS
    vmem = pl.BlockSpec(memory_space=pltpu.VMEM)
    anywhere = pl.BlockSpec(memory_space=pl.ANY)
    scratch = [
        pltpu.VMEM((nodes, columns), BF16),
        pltpu.VMEM((nodes, nodes), BF16),
        pltpu.VMEM((nodes, defl), BF16),
        pltpu.VMEM((4 * margin, nodes), BF16),
        pltpu.VMEM((nodes, 4 * margin), BF16),
        pltpu.VMEM((4 * margin, 4 * margin), BF16),
        pltpu.VMEM((4 * margin, defl), BF16),
        pltpu.VMEM((defl, 4 * margin), BF16),
        pltpu.VMEM((2 * defl, 4 * defl), BF16),
        pltpu.VMEM((2 * defl, defl), BF16),
        pltpu.VMEM((nodes, margin), F32),
        pltpu.VMEM((nodes, margin), F32),
        pltpu.VMEM((nodes, margin), F32),
        pltpu.VMEM((nodes, margin), F32),
        pltpu.VMEM((nodes, columns), F32),
        pltpu.VMEM((nodes, columns), F32),
        pltpu.VMEM((nodes, columns), F32),
        pltpu.VMEM((CHUNKS, defl, width), F32),
        pltpu.VMEM((CHUNKS, defl, width), F32),
        pltpu.VMEM((CHUNKS, defl, 2 * width), BF16),
        pltpu.VMEM((CHUNKS, 4 * margin, 2 * width), BF16),
        pltpu.VMEM((4, defl, margin), F32),
        pltpu.VMEM((4, defl, margin), F32),
        pltpu.VMEM((ITERS, CHUNKS, defl, width), F32),
        pltpu.VMEM((ITERS, CHUNKS, 4, defl, width), F32),
        pltpu.VMEM((ITERS, CHUNKS, 2, 4, margin, width), F32),
        pltpu.VMEM((ITERS, CHUNKS, 2, 4, margin, width), F32),
        pltpu.SemaphoreType.DMA,
        pltpu.SemaphoreType.DMA,
        pltpu.SemaphoreType.DMA((4,)),
        pltpu.SemaphoreType.DMA((4,)),
        pltpu.SemaphoreType.DMA((ITERS, CHUNKS, 3, 4)),
        pltpu.SemaphoreType.DMA((ITERS, CHUNKS, 3, 4)),
    ]
    sol, res = pl.pallas_call(
        functools.partial(kernel, mesh.shape["sub"], mesh.shape["grp"]),
        out_shape=(pltpu.VMEM((nodes, columns), F32), pltpu.VMEM((nodes, columns), BF16)),
        in_specs=[anywhere, pl.BlockSpec(memory_space=pl.ANY), vmem, vmem, vmem, vmem,
                  pl.BlockSpec(memory_space=pltpu.SMEM)],
        out_specs=(vmem, vmem),
        scratch_shapes=scratch,
        compiler_params=pltpu.CompilerParams(
            collective_id=0, has_side_effects=True, vmem_limit_bytes=56 * 1024 * 1024),
    )(rhs_field[0, 0], local_inverse[0, 0], stiff_diag[0], bonds[0], jnp.swapaxes(deflation[0, 0], 0, 1), margin_rows[0, 0],
      margin_count[0, 0])
    sol, res = pl.pallas_call(
        put_out,
        out_shape=(jax.ShapeDtypeStruct((nodes, columns), F32), jax.ShapeDtypeStruct((nodes, columns), BF16)),
        in_specs=[vmem, vmem],
        out_specs=(anywhere, anywhere),
        scratch_shapes=[pltpu.SemaphoreType.DMA((2,))],
        compiler_params=pltpu.CompilerParams(vmem_limit_bytes=1024 * 1024),
    )(pltpu.with_memory_space_constraint(sol, pltpu.VMEM), pltpu.with_memory_space_constraint(res, pltpu.VMEM))
    return sol[None, None], res[None, None]


def solution(mesh):
    placed = (
        P("sub", "grp", None, None),
        P("sub", "grp", None, None),
        P("sub", "grp", None),
        P("sub", "grp", None),
        P("sub", "grp", None, None),
        P("sub", "grp", None, None),
        P("sub", "grp", None),
    )
    return jax.shard_map(
        functools.partial(per_device, mesh),
        mesh=mesh,
        in_specs=placed,
        out_specs=(P("sub", "grp", None, None), P("sub", "grp", None, None)),
        check_vma=False,
    )
```

```python
import functools

import jax
import jax.numpy as jnp
from jax import lax
from jax.experimental import pallas as pl
from jax.experimental.pallas import tpu as pltpu
from jax.sharding import PartitionSpec as P

ITERS = 2
CHUNKS = 2

CHEB_FIRST = 0.4
CHEB_SECOND = 0.3
COUPLE_WEIGHT = 0.5

MESH = pl.DeviceIdType.MESH
F32 = jnp.float32
BF16 = jnp.bfloat16
NT = (((1,), (1,)), ((), ()))
SUB, GRP, ALL = (0, 1), (2, 3), (0, 1, 2, 3)


def dot(a, b):
    return jnp.dot(a, b, preferred_element_type=F32)


def dot_nt(a, b):
    return lax.dot_general(a, b, NT, preferred_element_type=F32)


def pair(x):
    high = x.astype(BF16)
    low = (x - high.astype(F32)).astype(BF16)
    return jnp.concatenate([high, low], axis=1)


def fold(x):
    width = x.shape[1] // 2
    return x[:, :width] + x[:, width:]


def one_hot(hit):
    return jnp.where(hit, 1.0, 0.0).astype(BF16)


def upright(row):
    size = row.shape[1]
    return jnp.broadcast_to(row, (size, size)).T


def kernel(
    subs, groups,
    rhs_hbm, inverse_hbm, diag_row, bond_row, basis_t, rows, count,
    sol_out, head_out, tail_out, spread, parts_out,
    rhs, inverse, gather, cross, edge_basis, edge_cols, tiles, own_tile,
    diag, inv_diag, bond_low, bond_high,
    resid, corr, total, own_part, pulled, came,
    edge_out, edge_in, coarse_out, coarse_in, margin_out, margin_in,
    edge_recv, send_sem, recv_sem,
):
    nodes, columns = rhs.shape
    defl = basis_t.shape[0]
    margin = rows.shape[1]
    width = columns // CHUNKS
    side = 2 * margin
    s, g = lax.axis_index("sub"), lax.axis_index("grp")
    has = [s > 0, s < subs - 1, g > 0, g < groups - 1]
    near = [(s - 1, g), (s + 1, g), (s, g - 1), (s, g + 1)]

    rhs_load = pltpu.make_async_copy(rhs_hbm, rhs, send_sem.at[1, 1, 0])
    rhs_load.start()

    barrier = pltpu.get_barrier_semaphore()
    for d in range(4):
        @pl.when(has[d])
        def _(d=d):
            pl.semaphore_signal(barrier, inc=1, device_id=near[d], device_id_type=MESH)

    def edge_copy(d):
        return pltpu.make_async_remote_copy(
            src_ref=edge_out.at[d], dst_ref=edge_in.at[d ^ 1],
            send_sem=send_sem.at[0, 1, d], recv_sem=edge_recv.at[d ^ 1],
            device_id=near[d], device_id_type=MESH)

    def coarse_copy(t, h, d):
        return pltpu.make_async_remote_copy(
            src_ref=coarse_out.at[t, h], dst_ref=coarse_in.at[t, h, d ^ 1],
            send_sem=send_sem.at[h, 3 * t % 2, d], recv_sem=recv_sem.at[h, 3 * t % 2, d ^ 1],
            device_id=near[d], device_id_type=MESH)

    def margin_copy(t, h, p, d):
        return pltpu.make_async_remote_copy(
            src_ref=margin_out.at[t, h, p, d], dst_ref=margin_in.at[t, h, p, d ^ 1],
            send_sem=send_sem.at[h, (3 * t + 1 + p) % 2, d], recv_sem=recv_sem.at[h, (3 * t + 1 + p) % 2, d ^ 1],
            device_id=near[d], device_id_type=MESH)

    def step_copy(k, h):
        if k % 3 == 0:
            return functools.partial(coarse_copy, k // 3, h)
        return functools.partial(margin_copy, k // 3, h, k % 3 - 1)

    def start(copy_to, dirs=ALL):
        for d in dirs:
            @pl.when(has[d])
            def _(d=d):
                copy_to(d).start()

    def send(k, h, dirs=ALL):
        for d in dirs:
            @pl.when(has[d])
            def _(d=d):
                if k >= 2:
                    step_copy(k - 2, h)(d).wait_send()
                step_copy(k, h)(d).start()

    def arrive(copy_to, dirs=ALL):
        for d in dirs:
            @pl.when(has[d])
            def _(d=d):
                copy_to(d ^ 1).wait_recv()

    def sent(copy_to):
        for d in range(4):
            @pl.when(has[d])
            def _(d=d):
                copy_to(d).wait_send()

    scatter, basis = spread.at[:, :4 * margin], spread.at[:, 4 * margin:]

    def cols(h):
        return pl.ds(h * width, width)

    def block(k):
        return pl.ds(k * side, side)

    row_values = rows[...].astype(F32)
    lane = lax.broadcasted_iota(jnp.int32, (margin, margin), 1).astype(F32)
    tall = []
    for d in range(4):
        tall.append(upright(row_values[d:d + 1]))
        for j in range(nodes // margin):
            gather[pl.ds(d * margin, margin), pl.ds(j * margin, margin)] = one_hot(tall[d] == lane + float(j * margin))
    edges = dot_nt(basis_t[...], gather[...])
    for d in range(4):
        edge_out[d] = edges[:, d * margin:(d + 1) * margin]
    rhs_load.wait()
    load = pltpu.make_async_copy(inverse_hbm, inverse, send_sem.at[1, 1, 1])
    load.start()
    first = dot(basis_t[...], rhs[...])
    for h in range(CHUNKS):
        coarse_out[0, h] = first[:, h * width:(h + 1) * width]

    pl.semaphore_wait(barrier, sum(h.astype(jnp.int32) for h in has))
    start(edge_copy)
    for h in range(CHUNKS):
        send(0, h)

    for d in range(4):
        @pl.when(jnp.logical_not(has[d]))
        def _(d=d):
            edge_in[d] = jnp.zeros_like(edge_in[d])
            for t in range(ITERS):
                for h in range(CHUNKS):
                    coarse_in[t, h, d] = jnp.zeros_like(coarse_in[t, h, d])
                    for p in range(2):
                        margin_in[t, h, p, d] = jnp.zeros_like(margin_in[t, h, p, d])

    basis[...] = basis_t[...].astype(F32).T.astype(BF16)
    edge_basis[...] = dot(gather[...], basis[...]).astype(BF16)
    for j in range(nodes // margin):
        part = pl.ds(j * margin, margin)
        tall_diag = upright(diag_row[:, j * margin:(j + 1) * margin])
        diag[part, :] = tall_diag
        inv_diag[part, :] = 1.0 / tall_diag
        bond_low[part, :] = upright(bond_row[:, j * margin:(j + 1) * margin])
    node = lax.broadcasted_iota(jnp.int32, (nodes, margin), 0).astype(F32)
    bonds = bond_low[...]
    bond_high[...] = jnp.where(node == float(nodes - 1), 0.0, pltpu.roll(bonds, nodes - 1, 0))
    bond_low[...] = jnp.where(node == 0.0, 0.0, bonds)

    def local_op(x):
        lanes = x.shape[1]
        return (diag[:, :lanes] * x - bond_low[:, :lanes] * pltpu.roll(x, 1, 0)
                - bond_high[:, :lanes] * pltpu.roll(x, nodes - 1, 0))

    def correct(t, h):
        wide = resid[:, cols(h)]
        value = corr[:, cols(h)] + wide * inv_diag[...]
        corr[:, cols(h)] = value
        taken = fold(dot(gather[...], pair(value)))
        for d in range(4):
            margin_out[t, h, 0, d] = taken[d * margin:(d + 1) * margin]

    load.wait()
    corr[...] = dot(inverse[...], rhs[...])
    for h in range(CHUNKS):
        resid[:, cols(h)] = rhs[:, h * width:(h + 1) * width].astype(F32)
    correct(0, 0)

    live = []
    spot = lax.broadcasted_iota(jnp.int32, (1, margin), 1)
    for d in range(4):
        live.append(spot < jnp.where(has[d], count[d], 0))
    for d in range(4):
        target = jnp.where(live[d], row_values[d:d + 1], -1.0)
        scatter[:, d * margin:(d + 1) * margin] = one_hot(node == target)
        for e in range(4):
            cross[pl.ds(e * margin, margin), pl.ds(d * margin, margin)] = one_hot(tall[e] == target)
        edge_cols[:, d * margin:(d + 1) * margin] = jnp.where(live[d], edge_out[d], 0.0).astype(BF16)

    def keep_stacked(ref, value):
        high = value.astype(BF16)
        ref[:defl] = high
        ref[defl:] = (value - high.astype(F32)).astype(BF16)

    def apply_stacked(ref, parts):
        both = dot(ref[...], parts)
        return fold(both[:defl]) + both[defl:, :width]

    pushed = pair(local_op(basis[...].astype(F32)))
    own = fold(dot(basis_t[...], pushed))
    eye = (lax.broadcasted_iota(jnp.int32, (defl, defl), 0)
           == lax.broadcasted_iota(jnp.int32, (defl, defl), 1)).astype(F32)
    keep_stacked(own_tile, (CHEB_FIRST + CHEB_SECOND) * eye - CHEB_FIRST * CHEB_SECOND * own)
    for h in range(CHUNKS):
        own_part[h] = apply_stacked(own_tile, pair(coarse_out[0, h]))

    arrive(edge_copy)
    sent(edge_copy)
    scale = CHEB_FIRST * CHEB_SECOND * COUPLE_WEIGHT
    keep_stacked(tiles, jnp.concatenate([
        scale * dot_nt(edge_cols[:, d * margin:(d + 1) * margin], edge_in[d].astype(BF16)) for d in range(4)], axis=1))

    def send_margin(t, h):
        arrive(functools.partial(coarse_copy, t, h), GRP)
        arrive(functools.partial(coarse_copy, t, h), SUB)
        parts = pair(own_part[h] + apply_stacked(tiles, pair(coarse_in[t, h].reshape(4 * defl, width))))
        came[h, 4 * margin:, :] = parts
        for k, dirs in enumerate((SUB, GRP)):
            taken = fold(dot(edge_basis[block(k), :], parts))
            for d in dirs:
                margin_out[t, h, 0, d] = margin_out[t, h, 0, d] + taken[(d % 2) * margin:(d % 2 + 1) * margin]
            send(3 * t + 1, h, dirs)

    def take(t, h, p, k):
        arrive(functools.partial(margin_copy, t, h, p), (SUB, GRP)[k])
        parts = pair(margin_in[t, h, p, 2 * k:2 * k + 2].reshape(side, width))
        came[h, block(k), :] = parts
        return parts

    def send_summed(t, h):
        taken = fold(dot(cross[:, side:], take(t, h, 0, 1)))
        for d in range(4):
            margin_out[t, h, 1, d] = margin_out[t, h, 0, d] + taken[d * margin:(d + 1) * margin]
        parts = take(t, h, 0, 0)
        for k, dirs in enumerate((SUB, GRP)):
            taken = fold(dot(cross[block(k), :side], parts))
            for d in dirs:
                margin_out[t, h, 1, d] = margin_out[t, h, 1, d] + taken[(d % 2) * margin:(d % 2 + 1) * margin]
            send(3 * t + 2, h, dirs)

    def add_up(t, h):
        summed = corr[:, cols(h)] + fold(dot(spread[...], came[h]))
        if t == 0:
            total[:, cols(h)] = summed
        else:
            total[:, cols(h)] = total[:, cols(h)] + summed
        if t == ITERS - 1:
            sol_out[:, cols(h)] = total[:, cols(h)]
        value = resid[:, cols(h)] - local_op(summed)
        resid[:, cols(h)] = value
        if t < ITERS - 1:
            pulled[h] = fold(dot(basis_t[...], pair(value)))

    def send_coarse(t, h):
        take(t, h, 1, 1)
        take(t, h, 1, 0)
        value = pulled[h] + COUPLE_WEIGHT * fold(dot(edge_cols[...], came[h, :4 * margin]))
        coarse_out[t + 1, h] = value
        send(3 * t + 3, h)

    def renew(t, h):
        own_part[h] = apply_stacked(own_tile, pair(coarse_out[t, h]))
        value = resid[:, cols(h)] + COUPLE_WEIGHT * fold(dot(scatter[...], came[h, :4 * margin]))
        resid[:, cols(h)] = value
        corr[:, cols(h)] = dot(inverse[...], value.astype(BF16))
        correct(t, h)

    for t in range(ITERS):
        for h in range(CHUNKS):
            send_margin(t, h)
            if t == 0 and h < CHUNKS - 1:
                correct(0, h + 1)
            if t > 0 and h == 0:
                renew(t, CHUNKS - 1)
        for h in range(CHUNKS):
            send_summed(t, h)
            add_up(t, h)
        for h in range(CHUNKS):
            if t < ITERS - 1:
                send_coarse(t, h)
                if h < CHUNKS - 1:
                    renew(t + 1, h)
            else:
                parts = take(t, h, 1, 1)
                value = resid[:, cols(h)] + COUPLE_WEIGHT * fold(dot(scatter[:, side:], parts))
                if h < CHUNKS - 1:
                    resid[:, cols(h)] = value
                else:
                    tail_out[...] = value
                parts = take(t, h, 1, 0)
                if h < CHUNKS - 1:
                    head_out[:, cols(h)] = (
                        resid[:, cols(h)] + COUPLE_WEIGHT * fold(dot(scatter[:, :side], parts))).astype(BF16)
                else:
                    parts_out[...] = parts

    for h in range(CHUNKS):
        for k in (3 * ITERS - 2, 3 * ITERS - 1):
            sent(step_copy(k, h))


def put_out(sol_in, head, tail, spread, parts, sol_out, res_out, last, sem):
    rest = head.shape[1]
    copies = [
        pltpu.make_async_copy(sol_in, sol_out, sem.at[0]),
        pltpu.make_async_copy(head, res_out.at[:, pl.ds(0, rest)], sem.at[1]),
        pltpu.make_async_copy(last, res_out.at[:, pl.ds(rest, last.shape[1])], sem.at[2]),
    ]
    copies[0].start()
    copies[1].start()
    last[...] = (tail[...] + COUPLE_WEIGHT * fold(dot(spread[:, :parts.shape[0]], parts[...]))).astype(BF16)
    copies[2].start()
    for copy in copies:
        copy.wait()


def per_device(mesh, rhs_field, local_inverse, stiff_diag, bonds, deflation, margin_rows, margin_count):
    nodes, columns = rhs_field.shape[2:]
    defl = deflation.shape[3]
    margin = margin_rows.shape[3]
    width = columns // CHUNKS
    vmem = pl.BlockSpec(memory_space=pltpu.VMEM)
    anywhere = pl.BlockSpec(memory_space=pl.ANY)
    scratch = [
        pltpu.VMEM((nodes, columns), BF16),
        pltpu.VMEM((nodes, nodes), BF16),
        pltpu.VMEM((4 * margin, nodes), BF16),
        pltpu.VMEM((4 * margin, 4 * margin), BF16),
        pltpu.VMEM((4 * margin, defl), BF16),
        pltpu.VMEM((defl, 4 * margin), BF16),
        pltpu.VMEM((2 * defl, 4 * defl), BF16),
        pltpu.VMEM((2 * defl, defl), BF16),
        pltpu.VMEM((nodes, margin), F32),
        pltpu.VMEM((nodes, margin), F32),
        pltpu.VMEM((nodes, margin), F32),
        pltpu.VMEM((nodes, margin), F32),
        pltpu.VMEM((nodes, columns), F32),
        pltpu.VMEM((nodes, columns), F32),
        pltpu.VMEM((nodes, columns), F32),
        pltpu.VMEM((CHUNKS, defl, width), F32),
        pltpu.VMEM((CHUNKS, defl, width), F32),
        pltpu.VMEM((CHUNKS, 4 * margin + defl, 2 * width), BF16),
        pltpu.VMEM((4, defl, margin), F32),
        pltpu.VMEM((4, defl, margin), F32),
        pltpu.VMEM((ITERS, CHUNKS, defl, width), F32),
        pltpu.VMEM((ITERS, CHUNKS, 4, defl, width), F32),
        pltpu.VMEM((ITERS, CHUNKS, 2, 4, margin, width), F32),
        pltpu.VMEM((ITERS, CHUNKS, 2, 4, margin, width), F32),
        pltpu.SemaphoreType.DMA((4,)),
        pltpu.SemaphoreType.DMA((CHUNKS, 2, 4)),
        pltpu.SemaphoreType.DMA((CHUNKS, 2, 4)),
    ]
    results = (
        pltpu.VMEM((nodes, columns), F32),
        pltpu.VMEM((nodes, columns - width), BF16),
        pltpu.VMEM((nodes, width), F32),
        pltpu.VMEM((nodes, 4 * margin + defl), BF16),
        pltpu.VMEM((2 * margin, 2 * width), BF16),
    )
    held = pl.pallas_call(
        functools.partial(kernel, mesh.shape["sub"], mesh.shape["grp"]),
        out_shape=results,
        in_specs=[anywhere, pl.BlockSpec(memory_space=pl.ANY), vmem, vmem, vmem, vmem,
                  pl.BlockSpec(memory_space=pltpu.SMEM)],
        out_specs=(vmem,) * len(results),
        scratch_shapes=scratch,
        compiler_params=pltpu.CompilerParams(
            collective_id=0, has_side_effects=True, vmem_limit_bytes=60 * 1024 * 1024),
    )(rhs_field[0, 0], local_inverse[0, 0], stiff_diag[0], bonds[0], jnp.swapaxes(deflation[0, 0], 0, 1), margin_rows[0, 0],
      margin_count[0, 0])
    sol, res = pl.pallas_call(
        put_out,
        out_shape=(jax.ShapeDtypeStruct((nodes, columns), F32), jax.ShapeDtypeStruct((nodes, columns), BF16)),
        in_specs=[vmem] * len(results),
        out_specs=(anywhere, anywhere),
        scratch_shapes=[pltpu.VMEM((nodes, width), BF16), pltpu.SemaphoreType.DMA((3,))],
        compiler_params=pltpu.CompilerParams(vmem_limit_bytes=8 * 1024 * 1024),
    )(*[pltpu.with_memory_space_constraint(x, pltpu.VMEM) for x in held])
    return sol[None, None], res[None, None]


def solution(mesh):
    placed = (
        P("sub", "grp", None, None),
        P("sub", "grp", None, None),
        P("sub", "grp", None),
        P("sub", "grp", None),
        P("sub", "grp", None, None),
        P("sub", "grp", None, None),
        P("sub", "grp", None),
    )
    return jax.shard_map(
        functools.partial(per_device, mesh),
        mesh=mesh,
        in_specs=placed,
        out_specs=(P("sub", "grp", None, None), P("sub", "grp", None, None)),
        check_vma=False,
    )
```

```python
import functools

import jax
import jax.numpy as jnp
from jax import lax
from jax.experimental import pallas as pl
from jax.experimental.pallas import tpu as pltpu
from jax.sharding import PartitionSpec as P

ITERS = 2
CHUNKS = 2

CHEB_FIRST = 0.4
CHEB_SECOND = 0.3
COUPLE_WEIGHT = 0.5

MESH = pl.DeviceIdType.MESH
F32 = jnp.float32
BF16 = jnp.bfloat16
NT = (((1,), (1,)), ((), ()))
SUB, GRP, ALL = (0, 1), (2, 3), (0, 1, 2, 3)


def dot(a, b):
    return jnp.dot(a, b, preferred_element_type=F32)


def dot_nt(a, b):
    return lax.dot_general(a, b, NT, preferred_element_type=F32)


def pair(x):
    high = x.astype(BF16)
    low = (x - high.astype(F32)).astype(BF16)
    return jnp.concatenate([high, low], axis=1)


def fold(x):
    width = x.shape[1] // 2
    return x[:, :width] + x[:, width:]


def one_hot(hit):
    return jnp.where(hit, 1.0, 0.0).astype(BF16)


def upright(row):
    size = row.shape[1]
    return jnp.broadcast_to(row, (size, size)).T


def kernel(
    subs, groups,
    rhs_hbm, inverse_hbm, diag_row, bond_row, basis_t, rows, count,
    sol_out, head_out, tail_out, spread, parts_out,
    rhs, inverse, gather, cross, edge_basis, edge_cols, tiles, own_tile,
    diag, inv_diag, bond_low, bond_high,
    resid, corr, total, own_part, pulled, came,
    edge_out, edge_in, coarse_out, coarse_in, margin_out, margin_in,
    edge_recv, send_sem, recv_sem,
):
    nodes, columns = rhs.shape
    defl = basis_t.shape[0]
    margin = rows.shape[1]
    width = columns // CHUNKS
    side = 2 * margin
    s, g = lax.axis_index("sub"), lax.axis_index("grp")
    has = [s > 0, s < subs - 1, g > 0, g < groups - 1]
    near = [(s - 1, g), (s + 1, g), (s, g - 1), (s, g + 1)]

    rhs_load = pltpu.make_async_copy(rhs_hbm, rhs, send_sem.at[1, 1, 0])
    rhs_load.start()

    barrier = pltpu.get_barrier_semaphore()
    for d in range(4):
        @pl.when(has[d])
        def _(d=d):
            pl.semaphore_signal(barrier, inc=1, device_id=near[d], device_id_type=MESH)

    def edge_copy(d):
        return pltpu.make_async_remote_copy(
            src_ref=edge_out.at[d], dst_ref=edge_in.at[d ^ 1],
            send_sem=send_sem.at[0, 1, d], recv_sem=edge_recv.at[d ^ 1],
            device_id=near[d], device_id_type=MESH)

    def coarse_copy(t, h, d):
        return pltpu.make_async_remote_copy(
            src_ref=coarse_out.at[t, h], dst_ref=coarse_in.at[t, h, d ^ 1],
            send_sem=send_sem.at[h, 0, d], recv_sem=recv_sem.at[h, 3 * t % 2, d ^ 1],
            device_id=near[d], device_id_type=MESH)

    def margin_copy(t, h, p, d):
        return pltpu.make_async_remote_copy(
            src_ref=margin_out.at[t, h, p, d], dst_ref=margin_in.at[t, h, p, d ^ 1],
            send_sem=send_sem.at[h, 0, d], recv_sem=recv_sem.at[h, (3 * t + 1 + p) % 2, d ^ 1],
            device_id=near[d], device_id_type=MESH)

    def step_copy(k, h):
        if k % 3 == 0:
            return functools.partial(coarse_copy, k // 3, h)
        return functools.partial(margin_copy, k // 3, h, k % 3 - 1)

    def start(copy_to, dirs=ALL):
        for d in dirs:
            @pl.when(has[d])
            def _(d=d):
                copy_to(d).start()

    def send(k, h, dirs=ALL):
        for d in dirs:
            @pl.when(has[d])
            def _(d=d):
                if k >= 1:
                    step_copy(k - 1, h)(d).wait_send()
                step_copy(k, h)(d).start()

    def arrive(copy_to, dirs=ALL):
        for d in dirs:
            @pl.when(has[d])
            def _(d=d):
                copy_to(d ^ 1).wait_recv()

    def sent(copy_to):
        for d in range(4):
            @pl.when(has[d])
            def _(d=d):
                copy_to(d).wait_send()

    scatter, basis = spread.at[:, :4 * margin], spread.at[:, 4 * margin:]

    def cols(h):
        return pl.ds(h * width, width)

    def block(k):
        return pl.ds(k * side, side)

    row_values = rows[...].astype(F32)
    lane = lax.broadcasted_iota(jnp.int32, (margin, margin), 1).astype(F32)
    tall = []
    for d in range(4):
        tall.append(upright(row_values[d:d + 1]))
        for j in range(nodes // margin):
            gather[pl.ds(d * margin, margin), pl.ds(j * margin, margin)] = one_hot(tall[d] == lane + float(j * margin))
    edges = dot_nt(basis_t[...], gather[...])
    for d in range(4):
        edge_out[d] = edges[:, d * margin:(d + 1) * margin]
    rhs_load.wait()
    load = pltpu.make_async_copy(inverse_hbm, inverse, send_sem.at[1, 1, 1])
    load.start()
    first = dot(basis_t[...], rhs[...])
    for h in range(CHUNKS):
        coarse_out[0, h] = first[:, h * width:(h + 1) * width]

    pl.semaphore_wait(barrier, sum(h.astype(jnp.int32) for h in has))
    start(edge_copy)
    send(0, 0)

    for d in range(4):
        @pl.when(jnp.logical_not(has[d]))
        def _(d=d):
            edge_in[d] = jnp.zeros_like(edge_in[d])
            for t in range(ITERS):
                for h in range(CHUNKS):
                    coarse_in[t, h, d] = jnp.zeros_like(coarse_in[t, h, d])
                    for p in range(2):
                        margin_in[t, h, p, d] = jnp.zeros_like(margin_in[t, h, p, d])

    basis[...] = basis_t[...].astype(F32).T.astype(BF16)
    edge_basis[...] = dot(gather[...], basis[...]).astype(BF16)
    for j in range(nodes // margin):
        part = pl.ds(j * margin, margin)
        tall_diag = upright(diag_row[:, j * margin:(j + 1) * margin])
        diag[part, :] = tall_diag
        inv_diag[part, :] = 1.0 / tall_diag
        bond_low[part, :] = upright(bond_row[:, j * margin:(j + 1) * margin])
    sent(edge_copy)
    for h in range(1, CHUNKS):
        send(0, h)
    node = lax.broadcasted_iota(jnp.int32, (nodes, margin), 0).astype(F32)
    bonds = bond_low[...]
    bond_high[...] = jnp.where(node == float(nodes - 1), 0.0, pltpu.roll(bonds, nodes - 1, 0))
    bond_low[...] = jnp.where(node == 0.0, 0.0, bonds)

    def local_op(x):
        lanes = x.shape[1]
        return (diag[:, :lanes] * x - bond_low[:, :lanes] * pltpu.roll(x, 1, 0)
                - bond_high[:, :lanes] * pltpu.roll(x, nodes - 1, 0))

    def correct(t, h):
        wide = resid[:, cols(h)]
        value = corr[:, cols(h)] + wide * inv_diag[...]
        corr[:, cols(h)] = value
        taken = fold(dot(gather[...], pair(value)))
        for d in range(4):
            margin_out[t, h, 0, d] = taken[d * margin:(d + 1) * margin]

    load.wait()
    corr[...] = dot(inverse[...], rhs[...])
    for h in range(CHUNKS):
        resid[:, cols(h)] = rhs[:, h * width:(h + 1) * width].astype(F32)
    correct(0, 0)

    live = []
    spot = lax.broadcasted_iota(jnp.int32, (1, margin), 1)
    for d in range(4):
        live.append(spot < jnp.where(has[d], count[d], 0))
    for d in range(4):
        target = jnp.where(live[d], row_values[d:d + 1], -1.0)
        scatter[:, d * margin:(d + 1) * margin] = one_hot(node == target)
        for e in range(4):
            cross[pl.ds(e * margin, margin), pl.ds(d * margin, margin)] = one_hot(tall[e] == target)
        edge_cols[:, d * margin:(d + 1) * margin] = jnp.where(live[d], edge_out[d], 0.0).astype(BF16)

    def keep_stacked(ref, value):
        high = value.astype(BF16)
        ref[:defl] = high
        ref[defl:] = (value - high.astype(F32)).astype(BF16)

    def apply_stacked(ref, parts):
        both = dot(ref[...], parts)
        return fold(both[:defl]) + both[defl:, :width]

    pushed = pair(local_op(basis[...].astype(F32)))
    own = fold(dot(basis_t[...], pushed))
    eye = (lax.broadcasted_iota(jnp.int32, (defl, defl), 0)
           == lax.broadcasted_iota(jnp.int32, (defl, defl), 1)).astype(F32)
    keep_stacked(own_tile, (CHEB_FIRST + CHEB_SECOND) * eye - CHEB_FIRST * CHEB_SECOND * own)
    for h in range(CHUNKS):
        own_part[h] = apply_stacked(own_tile, pair(coarse_out[0, h]))

    arrive(edge_copy)
    scale = CHEB_FIRST * CHEB_SECOND * COUPLE_WEIGHT
    keep_stacked(tiles, jnp.concatenate([
        scale * dot_nt(edge_cols[:, d * margin:(d + 1) * margin], edge_in[d].astype(BF16)) for d in range(4)], axis=1))

    def send_margin(t, h):
        arrive(functools.partial(coarse_copy, t, h), GRP)
        arrive(functools.partial(coarse_copy, t, h), SUB)
        parts = pair(own_part[h] + apply_stacked(tiles, pair(coarse_in[t, h].reshape(4 * defl, width))))
        came[h, 4 * margin:, :] = parts
        for k, dirs in enumerate((SUB, GRP)):
            taken = fold(dot(edge_basis[block(k), :], parts))
            for d in dirs:
                margin_out[t, h, 0, d] = margin_out[t, h, 0, d] + taken[(d % 2) * margin:(d % 2 + 1) * margin]
            send(3 * t + 1, h, dirs)

    def take(t, h, p, k):
        arrive(functools.partial(margin_copy, t, h, p), (SUB, GRP)[k])
        parts = pair(margin_in[t, h, p, 2 * k:2 * k + 2].reshape(side, width))
        came[h, block(k), :] = parts
        return parts

    def send_summed(t, h):
        taken = fold(dot(cross[:, side:], take(t, h, 0, 1)))
        for d in range(4):
            margin_out[t, h, 1, d] = margin_out[t, h, 0, d] + taken[d * margin:(d + 1) * margin]
        parts = take(t, h, 0, 0)
        for dirs in ((0,), (1,), GRP):
            taken = fold(dot(cross[pl.ds(dirs[0] * margin, len(dirs) * margin), :side], parts))
            for d in dirs:
                margin_out[t, h, 1, d] = margin_out[t, h, 1, d] + taken[(d - dirs[0]) * margin:(d - dirs[0] + 1) * margin]
            send(3 * t + 2, h, dirs)

    def add_up(t, h):
        summed = corr[:, cols(h)] + fold(dot(spread[...], came[h]))
        if t == 0:
            total[:, cols(h)] = summed
        else:
            total[:, cols(h)] = total[:, cols(h)] + summed
        if t == ITERS - 1:
            sol_out[:, cols(h)] = total[:, cols(h)]
        value = resid[:, cols(h)] - local_op(summed)
        resid[:, cols(h)] = value
        if t < ITERS - 1:
            pulled[h] = fold(dot(basis_t[...], pair(value)))

    def send_coarse(t, h):
        take(t, h, 1, 1)
        take(t, h, 1, 0)
        value = pulled[h] + COUPLE_WEIGHT * fold(dot(edge_cols[...], came[h, :4 * margin]))
        coarse_out[t + 1, h] = value
        send(3 * t + 3, h)

    def renew(t, h):
        own_part[h] = apply_stacked(own_tile, pair(coarse_out[t, h]))
        value = resid[:, cols(h)] + COUPLE_WEIGHT * fold(dot(scatter[...], came[h, :4 * margin]))
        resid[:, cols(h)] = value
        corr[:, cols(h)] = dot(inverse[...], value.astype(BF16))
        correct(t, h)

    for t in range(ITERS):
        for h in range(CHUNKS):
            send_margin(t, h)
            if t == 0 and h < CHUNKS - 1:
                correct(0, h + 1)
            if t > 0 and h == 0:
                renew(t, CHUNKS - 1)
        for h in range(CHUNKS):
            send_summed(t, h)
            add_up(t, h)
        for h in range(CHUNKS):
            if t < ITERS - 1:
                send_coarse(t, h)
                if h < CHUNKS - 1:
                    renew(t + 1, h)
            else:
                parts = take(t, h, 1, 1)
                value = resid[:, cols(h)] + COUPLE_WEIGHT * fold(dot(scatter[:, side:], parts))
                if h < CHUNKS - 1:
                    resid[:, cols(h)] = value
                else:
                    tail_out[...] = value
                parts = take(t, h, 1, 0)
                if h < CHUNKS - 1:
                    head_out[:, cols(h)] = (
                        resid[:, cols(h)] + COUPLE_WEIGHT * fold(dot(scatter[:, :side], parts))).astype(BF16)
                else:
                    parts_out[...] = parts

    for h in range(CHUNKS):
        sent(step_copy(3 * ITERS - 1, h))


def put_out(sol_in, head, tail, spread, parts, sol_out, res_out, last, sem):
    rest = head.shape[1]
    copies = [
        pltpu.make_async_copy(sol_in, sol_out, sem.at[0]),
        pltpu.make_async_copy(head, res_out.at[:, pl.ds(0, rest)], sem.at[1]),
        pltpu.make_async_copy(last, res_out.at[:, pl.ds(rest, last.shape[1])], sem.at[2]),
    ]
    copies[0].start()
    copies[1].start()
    last[...] = (tail[...] + COUPLE_WEIGHT * fold(dot(spread[:, :parts.shape[0]], parts[...]))).astype(BF16)
    copies[2].start()
    for copy in copies:
        copy.wait()


def per_device(mesh, rhs_field, local_inverse, stiff_diag, bonds, deflation, margin_rows, margin_count):
    nodes, columns = rhs_field.shape[2:]
    defl = deflation.shape[3]
    margin = margin_rows.shape[3]
    width = columns // CHUNKS
    vmem = pl.BlockSpec(memory_space=pltpu.VMEM)
    anywhere = pl.BlockSpec(memory_space=pl.ANY)
    scratch = [
        pltpu.VMEM((nodes, columns), BF16),
        pltpu.VMEM((nodes, nodes), BF16),
        pltpu.VMEM((4 * margin, nodes), BF16),
        pltpu.VMEM((4 * margin, 4 * margin), BF16),
        pltpu.VMEM((4 * margin, defl), BF16),
        pltpu.VMEM((defl, 4 * margin), BF16),
        pltpu.VMEM((2 * defl, 4 * defl), BF16),
        pltpu.VMEM((2 * defl, defl), BF16),
        pltpu.VMEM((nodes, margin), F32),
        pltpu.VMEM((nodes, margin), F32),
        pltpu.VMEM((nodes, margin), F32),
        pltpu.VMEM((nodes, margin), F32),
        pltpu.VMEM((nodes, columns), F32),
        pltpu.VMEM((nodes, columns), F32),
        pltpu.VMEM((nodes, columns), F32),
        pltpu.VMEM((CHUNKS, defl, width), F32),
        pltpu.VMEM((CHUNKS, defl, width), F32),
        pltpu.VMEM((CHUNKS, 4 * margin + defl, 2 * width), BF16),
        pltpu.VMEM((4, defl, margin), F32),
        pltpu.VMEM((4, defl, margin), F32),
        pltpu.VMEM((ITERS, CHUNKS, defl, width), F32),
        pltpu.VMEM((ITERS, CHUNKS, 4, defl, width), F32),
        pltpu.VMEM((ITERS, CHUNKS, 2, 4, margin, width), F32),
        pltpu.VMEM((ITERS, CHUNKS, 2, 4, margin, width), F32),
        pltpu.SemaphoreType.DMA((4,)),
        pltpu.SemaphoreType.DMA((CHUNKS, 2, 4)),
        pltpu.SemaphoreType.DMA((CHUNKS, 2, 4)),
    ]
    results = (
        pltpu.VMEM((nodes, columns), F32),
        pltpu.VMEM((nodes, columns - width), BF16),
        pltpu.VMEM((nodes, width), F32),
        pltpu.VMEM((nodes, 4 * margin + defl), BF16),
        pltpu.VMEM((2 * margin, 2 * width), BF16),
    )
    held = pl.pallas_call(
        functools.partial(kernel, mesh.shape["sub"], mesh.shape["grp"]),
        out_shape=results,
        in_specs=[anywhere, pl.BlockSpec(memory_space=pl.ANY), vmem, vmem, vmem, vmem,
                  pl.BlockSpec(memory_space=pltpu.SMEM)],
        out_specs=(vmem,) * len(results),
        scratch_shapes=scratch,
        compiler_params=pltpu.CompilerParams(
            collective_id=0, has_side_effects=True, vmem_limit_bytes=60 * 1024 * 1024),
    )(rhs_field[0, 0], local_inverse[0, 0], stiff_diag[0], bonds[0], jnp.swapaxes(deflation[0, 0], 0, 1), margin_rows[0, 0],
      margin_count[0, 0])
    sol, res = pl.pallas_call(
        put_out,
        out_shape=(jax.ShapeDtypeStruct((nodes, columns), F32), jax.ShapeDtypeStruct((nodes, columns), BF16)),
        in_specs=[vmem] * len(results),
        out_specs=(anywhere, anywhere),
        scratch_shapes=[pltpu.VMEM((nodes, width), BF16), pltpu.SemaphoreType.DMA((3,))],
        compiler_params=pltpu.CompilerParams(vmem_limit_bytes=8 * 1024 * 1024),
    )(*[pltpu.with_memory_space_constraint(x, pltpu.VMEM) for x in held])
    return sol[None, None], res[None, None]


def solution(mesh):
    placed = (
        P("sub", "grp", None, None),
        P("sub", "grp", None, None),
        P("sub", "grp", None),
        P("sub", "grp", None),
        P("sub", "grp", None, None),
        P("sub", "grp", None, None),
        P("sub", "grp", None),
    )
    return jax.shard_map(
        functools.partial(per_device, mesh),
        mesh=mesh,
        in_specs=placed,
        out_specs=(P("sub", "grp", None, None), P("sub", "grp", None, None)),
        check_vma=False,
    )
```

```python
import functools

import jax
import jax.numpy as jnp
from jax import lax
from jax.experimental import pallas as pl
from jax.experimental.pallas import tpu as pltpu
from jax.sharding import PartitionSpec as P

ITERS = 2
CHUNKS = 2

CHEB_FIRST = 0.4
CHEB_SECOND = 0.3
COUPLE_WEIGHT = 0.5

MESH = pl.DeviceIdType.MESH
F32 = jnp.float32
BF16 = jnp.bfloat16
NT = (((1,), (1,)), ((), ()))
SUB, GRP, ALL = (0, 1), (2, 3), (0, 1, 2, 3)


def dot(a, b):
    return jnp.dot(a, b, preferred_element_type=F32)


def dot_nt(a, b):
    return lax.dot_general(a, b, NT, preferred_element_type=F32)


def pair(x):
    high = x.astype(BF16)
    low = (x - high.astype(F32)).astype(BF16)
    return jnp.concatenate([high, low], axis=1)


def fold(x):
    width = x.shape[1] // 2
    return x[:, :width] + x[:, width:]


def one_hot(hit):
    return jnp.where(hit, 1.0, 0.0).astype(BF16)


def upright(row):
    size = row.shape[1]
    return jnp.broadcast_to(row, (size, size)).T


def kernel(
    subs, groups,
    rhs_hbm, inverse_hbm, diag_row, bond_row, basis_t, rows, count,
    sol_out, head_out, tail_out, spread, parts_out,
    rhs, inverse, gather, cross, edge_basis, edge_cols, tiles, own_tile,
    diag, inv_diag, bond_low, bond_high,
    resid, corr, total, own_part, pulled, came,
    edge_out, edge_in, coarse_out, coarse_in, margin_out, margin_in,
    load_sem, edge_recv, send_sem, recv_sem,
):
    nodes, columns = rhs.shape
    defl = basis_t.shape[0]
    margin = rows.shape[1]
    width = columns // CHUNKS
    side = 2 * margin
    s, g = lax.axis_index("sub"), lax.axis_index("grp")
    has = [s > 0, s < subs - 1, g > 0, g < groups - 1]
    near = [(s - 1, g), (s + 1, g), (s, g - 1), (s, g + 1)]

    rhs_load = pltpu.make_async_copy(rhs_hbm, rhs, send_sem.at[0, 0])
    rhs_load.start()

    barrier = pltpu.get_barrier_semaphore()
    for d in range(4):
        @pl.when(has[d])
        def _(d=d):
            pl.semaphore_signal(barrier, inc=1, device_id=near[d], device_id_type=MESH)

    def edge_copy(d):
        return pltpu.make_async_remote_copy(
            src_ref=edge_out.at[d], dst_ref=edge_in.at[d ^ 1],
            send_sem=send_sem.at[1, d], recv_sem=edge_recv.at[d ^ 1],
            device_id=near[d], device_id_type=MESH)

    def coarse_copy(t, h, d):
        return pltpu.make_async_remote_copy(
            src_ref=coarse_out.at[t, h], dst_ref=coarse_in.at[t, h, d ^ 1],
            send_sem=send_sem.at[h, d], recv_sem=recv_sem.at[h, 3 * t % 2, d ^ 1],
            device_id=near[d], device_id_type=MESH)

    def margin_copy(t, h, p, d):
        return pltpu.make_async_remote_copy(
            src_ref=margin_out.at[t, h, p, d], dst_ref=margin_in.at[t, h, p, d ^ 1],
            send_sem=send_sem.at[h, d], recv_sem=recv_sem.at[h, (3 * t + 1 + p) % 2, d ^ 1],
            device_id=near[d], device_id_type=MESH)

    def step_copy(k, h):
        if k % 3 == 0:
            return functools.partial(coarse_copy, k // 3, h)
        return functools.partial(margin_copy, k // 3, h, k % 3 - 1)

    def start(copy_to, dirs=ALL):
        for d in dirs:
            @pl.when(has[d])
            def _(d=d):
                copy_to(d).start()

    def send(k, h, dirs=ALL):
        for d in dirs:
            @pl.when(has[d])
            def _(d=d):
                if k >= 1:
                    step_copy(k - 1, h)(d).wait_send()
                step_copy(k, h)(d).start()

    def arrive(copy_to, dirs=ALL):
        for d in dirs:
            @pl.when(has[d])
            def _(d=d):
                copy_to(d ^ 1).wait_recv()

    def sent(copy_to):
        for d in range(4):
            @pl.when(has[d])
            def _(d=d):
                copy_to(d).wait_send()

    scatter, basis = spread.at[:, :4 * margin], spread.at[:, 4 * margin:]

    def cols(h):
        return pl.ds(h * width, width)

    def block(k):
        return pl.ds(k * side, side)

    row_values = rows[...].astype(F32)
    lane = lax.broadcasted_iota(jnp.int32, (margin, margin), 1).astype(F32)
    tall = []
    for d in range(4):
        tall.append(upright(row_values[d:d + 1]))
        for j in range(nodes // margin):
            gather[pl.ds(d * margin, margin), pl.ds(j * margin, margin)] = one_hot(tall[d] == lane + float(j * margin))
    edges = dot_nt(basis_t[...], gather[...])
    for d in range(4):
        edge_out[d] = edges[:, d * margin:(d + 1) * margin]
    rhs_load.wait()
    load = pltpu.make_async_copy(inverse_hbm, inverse, load_sem)
    load.start()
    first = dot(basis_t[...], rhs[...])
    for h in range(CHUNKS):
        coarse_out[0, h] = first[:, h * width:(h + 1) * width]

    pl.semaphore_wait(barrier, sum(h.astype(jnp.int32) for h in has))
    start(edge_copy)
    send(0, 0)

    for d in range(4):
        @pl.when(jnp.logical_not(has[d]))
        def _(d=d):
            edge_in[d] = jnp.zeros_like(edge_in[d])
            for t in range(ITERS):
                for h in range(CHUNKS):
                    coarse_in[t, h, d] = jnp.zeros_like(coarse_in[t, h, d])
                    for p in range(2):
                        margin_in[t, h, p, d] = jnp.zeros_like(margin_in[t, h, p, d])

    basis[...] = basis_t[...].astype(F32).T.astype(BF16)
    edge_basis[...] = dot(gather[...], basis[...]).astype(BF16)
    for j in range(nodes // margin):
        part = pl.ds(j * margin, margin)
        tall_diag = upright(diag_row[:, j * margin:(j + 1) * margin])
        diag[part, :] = tall_diag
        inv_diag[part, :] = 1.0 / tall_diag
        bond_low[part, :] = upright(bond_row[:, j * margin:(j + 1) * margin])
    sent(edge_copy)
    for h in range(1, CHUNKS):
        send(0, h)
    node = lax.broadcasted_iota(jnp.int32, (nodes, margin), 0).astype(F32)
    bonds = bond_low[...]
    bond_high[...] = jnp.where(node == float(nodes - 1), 0.0, pltpu.roll(bonds, nodes - 1, 0))
    bond_low[...] = jnp.where(node == 0.0, 0.0, bonds)

    def local_op(x):
        lanes = x.shape[1]
        return (diag[:, :lanes] * x - bond_low[:, :lanes] * pltpu.roll(x, 1, 0)
                - bond_high[:, :lanes] * pltpu.roll(x, nodes - 1, 0))

    def correct(t, h):
        wide = resid[:, cols(h)]
        value = corr[:, cols(h)] + wide * inv_diag[...]
        corr[:, cols(h)] = value
        taken = fold(dot(gather[...], pair(value)))
        for d in range(4):
            margin_out[t, h, 0, d] = taken[d * margin:(d + 1) * margin]

    load.wait()
    corr[...] = dot(inverse[...], rhs[...])
    for h in range(CHUNKS):
        resid[:, cols(h)] = rhs[:, h * width:(h + 1) * width].astype(F32)
    correct(0, 0)

    live = []
    spot = lax.broadcasted_iota(jnp.int32, (1, margin), 1)
    for d in range(4):
        live.append(spot < jnp.where(has[d], count[d], 0))
    for d in range(4):
        target = jnp.where(live[d], row_values[d:d + 1], -1.0)
        scatter[:, d * margin:(d + 1) * margin] = one_hot(node == target)
        for e in range(4):
            cross[pl.ds(e * margin, margin), pl.ds(d * margin, margin)] = one_hot(tall[e] == target)
        edge_cols[:, d * margin:(d + 1) * margin] = jnp.where(live[d], edge_out[d], 0.0).astype(BF16)

    def keep_stacked(ref, value):
        high = value.astype(BF16)
        ref[:defl] = high
        ref[defl:] = (value - high.astype(F32)).astype(BF16)

    def apply_stacked(ref, parts):
        both = dot(ref[...], parts)
        return fold(both[:defl]) + both[defl:, :width]

    pushed = pair(local_op(basis[...].astype(F32)))
    own = fold(dot(basis_t[...], pushed))
    eye = (lax.broadcasted_iota(jnp.int32, (defl, defl), 0)
           == lax.broadcasted_iota(jnp.int32, (defl, defl), 1)).astype(F32)
    keep_stacked(own_tile, (CHEB_FIRST + CHEB_SECOND) * eye - CHEB_FIRST * CHEB_SECOND * own)
    for h in range(CHUNKS):
        own_part[h] = apply_stacked(own_tile, pair(coarse_out[0, h]))

    arrive(edge_copy)
    scale = CHEB_FIRST * CHEB_SECOND * COUPLE_WEIGHT
    keep_stacked(tiles, jnp.concatenate([
        scale * dot_nt(edge_cols[:, d * margin:(d + 1) * margin], edge_in[d].astype(BF16)) for d in range(4)], axis=1))

    def send_margin(t, h):
        arrive(functools.partial(coarse_copy, t, h), GRP)
        arrive(functools.partial(coarse_copy, t, h), SUB)
        parts = pair(own_part[h] + apply_stacked(tiles, pair(coarse_in[t, h].reshape(4 * defl, width))))
        came[h, 4 * margin:, :] = parts
        for k, dirs in enumerate((SUB, GRP)):
            taken = fold(dot(edge_basis[block(k), :], parts))
            for d in dirs:
                margin_out[t, h, 0, d] = margin_out[t, h, 0, d] + taken[(d % 2) * margin:(d % 2 + 1) * margin]
            send(3 * t + 1, h, dirs)

    def take(t, h, p, k):
        arrive(functools.partial(margin_copy, t, h, p), (SUB, GRP)[k])
        parts = pair(margin_in[t, h, p, 2 * k:2 * k + 2].reshape(side, width))
        came[h, block(k), :] = parts
        return parts

    def send_summed(t, h):
        taken = fold(dot(cross[:, side:], take(t, h, 0, 1)))
        for d in range(4):
            margin_out[t, h, 1, d] = margin_out[t, h, 0, d] + taken[d * margin:(d + 1) * margin]
        parts = take(t, h, 0, 0)
        for dirs in ((0,), (1,), GRP):
            taken = fold(dot(cross[pl.ds(dirs[0] * margin, len(dirs) * margin), :side], parts))
            for d in dirs:
                margin_out[t, h, 1, d] = margin_out[t, h, 1, d] + taken[(d - dirs[0]) * margin:(d - dirs[0] + 1) * margin]
            send(3 * t + 2, h, dirs)

    def add_up(t, h):
        summed = corr[:, cols(h)] + fold(dot(spread[...], came[h]))
        if t == 0:
            total[:, cols(h)] = summed
        else:
            total[:, cols(h)] = total[:, cols(h)] + summed
        if t == ITERS - 1:
            sol_out[:, cols(h)] = total[:, cols(h)]
        value = resid[:, cols(h)] - local_op(summed)
        resid[:, cols(h)] = value
        if t < ITERS - 1:
            pulled[h] = fold(dot(basis_t[...], pair(value)))

    def send_coarse(t, h):
        take(t, h, 1, 1)
        take(t, h, 1, 0)
        value = pulled[h] + COUPLE_WEIGHT * fold(dot(edge_cols[...], came[h, :4 * margin]))
        coarse_out[t + 1, h] = value
        send(3 * t + 3, h)

    def renew(t, h):
        own_part[h] = apply_stacked(own_tile, pair(coarse_out[t, h]))
        value = resid[:, cols(h)] + COUPLE_WEIGHT * fold(dot(scatter[...], came[h, :4 * margin]))
        resid[:, cols(h)] = value
        corr[:, cols(h)] = dot(inverse[...], value.astype(BF16))
        correct(t, h)

    for t in range(ITERS):
        for h in range(CHUNKS):
            send_margin(t, h)
            if t == 0 and h < CHUNKS - 1:
                correct(0, h + 1)
            if t > 0 and h == 0:
                renew(t, CHUNKS - 1)
        for h in range(CHUNKS):
            send_summed(t, h)
            add_up(t, h)
        for h in range(CHUNKS):
            if t < ITERS - 1:
                send_coarse(t, h)
                if h < CHUNKS - 1:
                    renew(t + 1, h)
            else:
                parts = take(t, h, 1, 1)
                value = resid[:, cols(h)] + COUPLE_WEIGHT * fold(dot(scatter[:, side:], parts))
                if h < CHUNKS - 1:
                    resid[:, cols(h)] = value
                else:
                    tail_out[...] = value
                parts = take(t, h, 1, 0)
                if h < CHUNKS - 1:
                    head_out[:, cols(h)] = (
                        resid[:, cols(h)] + COUPLE_WEIGHT * fold(dot(scatter[:, :side], parts))).astype(BF16)
                else:
                    parts_out[...] = parts

    for h in range(CHUNKS):
        sent(step_copy(3 * ITERS - 1, h))


def put_out(sol_in, head, tail, spread, parts, sol_out, res_out, last, sem):
    rest = head.shape[1]
    copies = [
        pltpu.make_async_copy(sol_in, sol_out, sem.at[0]),
        pltpu.make_async_copy(head, res_out.at[:, pl.ds(0, rest)], sem.at[1]),
        pltpu.make_async_copy(last, res_out.at[:, pl.ds(rest, last.shape[1])], sem.at[2]),
    ]
    copies[0].start()
    copies[1].start()
    last[...] = (tail[...] + COUPLE_WEIGHT * fold(dot(spread[:, :parts.shape[0]], parts[...]))).astype(BF16)
    copies[2].start()
    for copy in copies:
        copy.wait()


def per_device(mesh, rhs_field, local_inverse, stiff_diag, bonds, deflation, margin_rows, margin_count):
    nodes, columns = rhs_field.shape[2:]
    defl = deflation.shape[3]
    margin = margin_rows.shape[3]
    width = columns // CHUNKS
    vmem = pl.BlockSpec(memory_space=pltpu.VMEM)
    anywhere = pl.BlockSpec(memory_space=pl.ANY)
    scratch = [
        pltpu.VMEM((nodes, columns), BF16),
        pltpu.VMEM((nodes, nodes), BF16),
        pltpu.VMEM((4 * margin, nodes), BF16),
        pltpu.VMEM((4 * margin, 4 * margin), BF16),
        pltpu.VMEM((4 * margin, defl), BF16),
        pltpu.VMEM((defl, 4 * margin), BF16),
        pltpu.VMEM((2 * defl, 4 * defl), BF16),
        pltpu.VMEM((2 * defl, defl), BF16),
        pltpu.VMEM((nodes, margin), F32),
        pltpu.VMEM((nodes, margin), F32),
        pltpu.VMEM((nodes, margin), F32),
        pltpu.VMEM((nodes, margin), F32),
        pltpu.VMEM((nodes, columns), F32),
        pltpu.VMEM((nodes, columns), F32),
        pltpu.VMEM((nodes, columns), F32),
        pltpu.VMEM((CHUNKS, defl, width), F32),
        pltpu.VMEM((CHUNKS, defl, width), F32),
        pltpu.VMEM((CHUNKS, 4 * margin + defl, 2 * width), BF16),
        pltpu.VMEM((4, defl, margin), F32),
        pltpu.VMEM((4, defl, margin), F32),
        pltpu.VMEM((ITERS, CHUNKS, defl, width), F32),
        pltpu.VMEM((ITERS, CHUNKS, 4, defl, width), F32),
        pltpu.VMEM((ITERS, CHUNKS, 2, 4, margin, width), F32),
        pltpu.VMEM((ITERS, CHUNKS, 2, 4, margin, width), F32),
        pltpu.SemaphoreType.DMA,
        pltpu.SemaphoreType.DMA((4,)),
        pltpu.SemaphoreType.DMA((CHUNKS, 4)),
        pltpu.SemaphoreType.DMA((CHUNKS, 2, 4)),
    ]
    results = (
        pltpu.VMEM((nodes, columns), F32),
        pltpu.VMEM((nodes, columns - width), BF16),
        pltpu.VMEM((nodes, width), F32),
        pltpu.VMEM((nodes, 4 * margin + defl), BF16),
        pltpu.VMEM((2 * margin, 2 * width), BF16),
    )
    held = pl.pallas_call(
        functools.partial(kernel, mesh.shape["sub"], mesh.shape["grp"]),
        out_shape=results,
        in_specs=[anywhere, pl.BlockSpec(memory_space=pl.ANY), vmem, vmem, vmem, vmem,
                  pl.BlockSpec(memory_space=pltpu.SMEM)],
        out_specs=(vmem,) * len(results),
        scratch_shapes=scratch,
        compiler_params=pltpu.CompilerParams(
            collective_id=0, has_side_effects=True, vmem_limit_bytes=60 * 1024 * 1024),
    )(rhs_field[0, 0], local_inverse[0, 0], stiff_diag[0], bonds[0], jnp.swapaxes(deflation[0, 0], 0, 1), margin_rows[0, 0],
      margin_count[0, 0])
    sol, res = pl.pallas_call(
        put_out,
        out_shape=(jax.ShapeDtypeStruct((nodes, columns), F32), jax.ShapeDtypeStruct((nodes, columns), BF16)),
        in_specs=[vmem] * len(results),
        out_specs=(anywhere, anywhere),
        scratch_shapes=[pltpu.VMEM((nodes, width), BF16), pltpu.SemaphoreType.DMA((3,))],
        compiler_params=pltpu.CompilerParams(vmem_limit_bytes=8 * 1024 * 1024),
    )(*[pltpu.with_memory_space_constraint(x, pltpu.VMEM) for x in held])
    return sol[None, None], res[None, None]


def solution(mesh):
    placed = (
        P("sub", "grp", None, None),
        P("sub", "grp", None, None),
        P("sub", "grp", None),
        P("sub", "grp", None),
        P("sub", "grp", None, None),
        P("sub", "grp", None, None),
        P("sub", "grp", None),
    )
    return jax.shard_map(
        functools.partial(per_device, mesh),
        mesh=mesh,
        in_specs=placed,
        out_specs=(P("sub", "grp", None, None), P("sub", "grp", None, None)),
        check_vma=False,
    )
```
